32 devices in a mesh: grp: 2 (over x), ctx: 8 (over z, y), head: 2 (over core).
Axes of the slice: x: 2, y: 2, z: 4, core: 2. Of those that a mesh axis runs over, the one named last changes fastest.
Arguments:
- queries: bfloat16 [3072, 16, 128], P(('grp', 'ctx'), 'head'), parts along dimension 0
- key_vecs: bfloat16 [3072, 16, 128], P(('grp', 'ctx'), 'head'), parts along dimension 0
- value_vecs: bfloat16 [3072, 16, 128], P(('grp', 'ctx'), 'head'), parts along dimension 0, may hold values from -6 to 6
- out_grad: bfloat16 [3072, 16, 128], P(('grp', 'ctx'), 'head'), parts along dimension 0, may hold values from -6 to 6
- doc_ids: int32 [3072], P('grp'), parts along dimension 0, may hold values from 0 to 5, never falling along the last dimension, each value on 1 to 960 neighbouring positions
Outputs:
- attn_out: bfloat16 [3072, 16, 128], P(('grp', 'ctx'), 'head'), parts along dimension 0
- query_grad: bfloat16 [3072, 16, 128], P(('grp', 'ctx'), 'head'), parts along dimension 0
- key_grad: bfloat16 [3072, 16, 128], P(('grp', 'ctx'), 'head'), parts along dimension 0
- value_grad: bfloat16 [3072, 16, 128], P(('grp', 'ctx'), 'head'), parts along dimension 0
The draws below stay inside these ranges and needn't reach their ends.
There are 2 independent parts, one for each index of `grp`. The reference program is written for one: setup_inputs(seed, part) draws one part's arguments, and reference() takes and returns one part's arrays. A program takes and returns all parts, laid end to end along the dimension named above; each array names one. Nothing has to cross between parts.
Inputs may be any that keep to these rules, and one draw needn't show every extreme that they name: doc_ids never fall along the sequence; every document has 1 to 960 tokens and one has exactly 960.
All inputs are finite; a program needn't handle non-finite values.
Results may differ from the reference program's by a relative error of at most 0.035.
Values may be sent and summed in bfloat16 or wider, within the bound.
No kernel may reach another device: no remote copies, remote signals or barrier semaphores. Data moves between devices by JAX's collectives and lax.ppermute only.
A program may use at most 128 MiB of HBM per device.

```python
import math
import jax
import jax.numpy as jnp
import numpy as np
from jax import lax

DH = 128
HEADS = 16
S_DEV = 192
DOCS = 6
TOKENS = 1536
DOC_MOST = 960
N_CTX = 8


def paired_vectors(key):
    base = jax.random.fold_in(key, 7)
    key_query, key_key = jax.random.split(base, 2)
    shape = (TOKENS, HEADS, DH)
    query_vals = jnp.clip(jax.random.normal(key_query, shape, jnp.float32), -6.0, 6.0)
    key_vals = jnp.clip(jax.random.normal(key_key, shape, jnp.float32), -6.0, 6.0)
    return (query_vals, key_vals)


def draw_queries(key, part):
    return paired_vectors(key)[0].astype(jnp.bfloat16)


def draw_key_vecs(key, part):
    return paired_vectors(key)[1].astype(jnp.bfloat16)


def block_scale(key, dims, pieces, low, top_value):
    factor_of = 1.0
    for dim, parts in pieces:
        draws = jax.random.uniform(jax.random.fold_in(jax.random.fold_in(key, 6), dim), (parts,), jnp.float32, low / len(pieces), top_value / len(pieces))
        factor_of = factor_of * jnp.repeat(jnp.exp(draws), dims[dim] // parts).reshape((-1,) + (1,) * (len(dims) - 1 - dim))
    return factor_of


def profile(count, total, limit, slope):
    weights = [(1 << 20) // math.isqrt(rank ** slope) + 1 for rank in range(2, count + 1)]
    spare, given = total - limit - (count - 1), [1] * (count - 1)
    while spare > 0:
        movable = [i for i in range(count - 1) if given[i] < limit]
        pool, budget = sum([weights[i] for i in movable]), spare
        for i in movable:
            more = min(limit - given[i], max(1, budget * weights[i] // pool), spare)
            given[i] = given[i] + more
            spare = spare - more
    return np.array([limit] + given)


def uneven(stream_key, number_of, total, limit, slope):
    if number_of == 2:
        one = jax.random.randint(stream_key, (), max(1, total - limit), min(limit, total - 1) + 1)
        return jnp.stack([one, total - one])
    sizes = jnp.asarray(profile(number_of, total, limit, slope), jnp.int32)
    couples = (number_of - 1) // 2
    giver, taker = sizes[1:1 + 2 * couples:2], sizes[2:2 + 2 * couples:2]
    room = jnp.minimum(giver - 1, limit - taker)
    moved = jax.random.randint(jax.random.fold_in(stream_key, 1), (couples,), 0, 1 << 20) % (room + 1)
    sizes = sizes.at[1:1 + 2 * couples:2].set(giver - moved).at[2:2 + 2 * couples:2].set(taker + moved)
    return sizes[jax.random.permutation(jax.random.fold_in(stream_key, 2), number_of)]


def scatter_about(own_key, shape, spread, bound, pieces=(), held_as=jnp.bfloat16):
    values = jax.random.normal(own_key, shape, jnp.float32) * spread
    if len(pieces) > 0:
        values = block_scale(own_key, shape, pieces, -0.22, 0.18) * values
    return jnp.clip(values, min=-bound, max=bound).astype(held_as)


def setup_inputs(seed: int = 0, part: int = 0) -> dict:
    key_of = jax.random.split(jax.random.key(seed), 6)
    part_splits = jax.random.split(jax.random.fold_in(key_of[5], part), 6)
    return {
        "queries": draw_queries(jax.random.fold_in(jax.random.fold_in(key_of[5], part), 71), part),
        "key_vecs": draw_key_vecs(jax.random.fold_in(jax.random.fold_in(key_of[5], part), 71), part),
        "value_vecs": scatter_about(part_splits[2], (TOKENS, HEADS, DH), 1.0, 6.0, ((0, 8), (1, 2))),
        "out_grad": scatter_about(part_splits[3], (TOKENS, HEADS, DH), 1.0, 6.0, ((0, 8), (1, 2))),
        "doc_ids": jnp.searchsorted(jnp.cumsum(uneven(part_splits[4], DOCS, TOKENS, DOC_MOST, 2)), jnp.arange(TOKENS), side="right").astype(jnp.int32),
    }


def one_head(operands, visible):
    query_rows, key_rows, value_rows, grad_rows = operands
    scaling = DH ** -0.5
    scores = jnp.dot(query_rows, key_rows.T, preferred_element_type=jnp.float32) * scaling
    largest = jnp.max(jnp.where(visible, scores, -1e30), axis=-1)
    weights = jnp.where(visible, jnp.exp(scores - largest[:, None]), 0.0)
    lse = largest + jnp.log(jnp.sum(weights, axis=-1))
    probs = jnp.where(visible, jnp.exp(scores - lse[:, None]), 0.0).astype(jnp.bfloat16)
    attn_out = jnp.dot(probs, value_rows, preferred_element_type=jnp.float32).astype(jnp.bfloat16)
    delta = jnp.sum(grad_rows.astype(jnp.float32) * attn_out.astype(jnp.float32), axis=-1)
    dprobs = jnp.dot(grad_rows, value_rows.T, preferred_element_type=jnp.float32)
    dscores = (probs.astype(jnp.float32) * (dprobs - delta[:, None])).astype(jnp.bfloat16)
    query_grad = (scaling * jnp.dot(dscores, key_rows, preferred_element_type=jnp.float32)).astype(jnp.bfloat16)
    key_grad = (scaling * jnp.dot(dscores.T, query_rows, preferred_element_type=jnp.float32)).astype(jnp.bfloat16)
    value_grad = jnp.dot(probs.T, grad_rows, preferred_element_type=jnp.float32).astype(jnp.bfloat16)
    return attn_out, query_grad, key_grad, value_grad


def stored_position(rows, shard_rows, shard_count):
    half_rows = shard_rows // 2
    shard = rows // shard_rows
    within = rows % shard_rows
    return jnp.where(within < half_rows, shard * half_rows + within,
                     (2 * shard_count - 1 - shard) * half_rows + within - half_rows).astype(jnp.int32)


def reference(queries, key_vecs, value_vecs, out_grad, doc_ids):
    rows = jnp.arange(TOKENS, dtype=jnp.int32)
    position = stored_position(rows, S_DEV, N_CTX)
    row_doc = jnp.take(doc_ids, position)
    visible = (row_doc[None, :] == row_doc[:, None]) & (position[None, :] <= position[:, None])
    stacked = tuple(jnp.transpose(array, (1, 0, 2)) for array in (queries, key_vecs, value_vecs, out_grad))
    results = lax.map(lambda operands: one_head(operands, visible), stacked)
    attn_out, query_grad, key_grad, value_grad = tuple(jnp.transpose(array, (1, 0, 2)) for array in results)
    return (attn_out, query_grad, key_grad, value_grad)
```

```python
import functools
import math

import jax
import jax.numpy as jnp
from jax import lax
from jax.experimental import pallas as pl
from jax.experimental.pallas import tpu as pltpu
from jax.sharding import PartitionSpec as P

TILE = 256
HIDDEN = -1e30


def partner_order(count):
    return sorted(range(1, count), key=lambda d: (-(d.bit_length()), -d))


def nt_dot(a, b):
    return lax.dot_general(a, b, (((1,), (1,)), ((), ())), preferred_element_type=jnp.float32)


def dot(a, b):
    return jnp.dot(a, b, preferred_element_type=jnp.float32)


def attention_kernel(count, tile_most, *refs):
    scalars, start_ref = refs[0], refs[1]
    ins = refs[2 : 2 + count]
    outs = refs[2 + count : 2 + 2 * count]
    rows, key_t, value_t, scores, weights, key_sum, value_sum, result = refs[2 + 2 * count :]
    me = scalars[0]
    shard_rows = ins[0].shape[1]
    half = shard_rows // 2
    tokens = rows.shape[1]
    head_size = rows.shape[2]
    tile = TILE
    scaling = head_size ** (-0.5)
    exponent = scaling * math.log2(math.e)

    for d in range(count):
        shard = me ^ d
        low = pl.multiple_of(shard * half, half)
        high = pl.multiple_of((2 * count - 1 - shard) * half, half)
        for t in range(4):
            rows[t, pl.ds(low, half), :] = ins[d][t, :half, :]
            rows[t, pl.ds(high, half), :] = ins[d][t, half:, :]
    for b in range(tokens // tile):
        block = pl.ds(b * tile, tile)
        key_t[:, block] = rows[1, block, :].T
        value_t[:, block] = rows[2, block, :].T
    key_sum[...] = jnp.zeros_like(key_sum)
    value_sum[...] = jnp.zeros_like(value_sum)

    def query_tile(size, j):
        q_at = pl.multiple_of(j * tile, tile)
        k_at = pl.multiple_of((j - (size - 1)) * tile, tile)
        q_blk = rows[0, pl.ds(q_at, tile), :]
        start = start_ref[:, pl.ds(q_at, tile)]
        best = jnp.full((1, tile), HIDDEN, jnp.float32)
        for i in range(size):
            s = nt_dot(rows[1, pl.ds(k_at + i * tile, tile), :], q_blk) * exponent
            k_pos = lax.broadcasted_iota(jnp.int32, (tile, tile), 0) + (k_at + i * tile)
            seen = k_pos >= start
            if i == size - 1:
                q_pos = lax.broadcasted_iota(jnp.int32, (tile, tile), 1) + q_at
                seen = seen & (k_pos <= q_pos)
            s = jnp.where(seen, s, HIDDEN)
            scores[i * tile : (i + 1) * tile, :] = s
            best = jnp.maximum(best, jnp.max(s, axis=0, keepdims=True))
        total = jnp.zeros((1, tile), jnp.float32)
        for i in range(size):
            e = jnp.exp2(scores[i * tile : (i + 1) * tile, :] - best)
            total = total + jnp.sum(e, axis=0, keepdims=True)
            weights[i * tile : (i + 1) * tile, :] = e.astype(jnp.bfloat16)
        inverse = 1.0 / total
        out_t = dot(value_t[:, pl.ds(k_at, size * tile)], weights[: size * tile, :]) * inverse
        out = out_t.astype(jnp.bfloat16)
        result[0, pl.ds(q_at, tile), :] = out_t.T.astype(jnp.bfloat16)
        grad_t = rows[3, pl.ds(q_at, tile), :].astype(jnp.float32).T * inverse
        delta = jnp.sum(grad_t * out.astype(jnp.float32), axis=0, keepdims=True)
        grad_tb = grad_t.astype(jnp.bfloat16)
        grad = grad_t.T.astype(jnp.bfloat16)
        query_t = jnp.zeros((head_size, tile), jnp.float32)
        for i in range(size):
            keys = pl.ds(k_at + i * tile, tile)
            e = weights[i * tile : (i + 1) * tile, :]
            value_sum[keys, :] += dot(e, grad)
            dprobs = dot(rows[2, keys, :], grad_tb)
            ds = (e.astype(jnp.float32) * (dprobs - delta)).astype(jnp.bfloat16)
            key_sum[keys, :] += dot(ds, q_blk)
            query_t = query_t + dot(key_t[:, keys], ds)
        result[1, pl.ds(q_at, tile), :] = (query_t * scaling).T.astype(jnp.bfloat16)

    @pl.loop(0, tokens // tile)
    def _(j):
        size = j - scalars[1 + j] + 1
        for n in range(1, tile_most + 1):

            @pl.when(size == n)
            def _(n=n):
                query_tile(n, j)

    result[2] = (key_sum[...] * scaling).astype(jnp.bfloat16)
    result[3] = value_sum[...].astype(jnp.bfloat16)
    for d in range(count):
        shard = me ^ d
        low = pl.multiple_of(shard * half, half)
        high = pl.multiple_of((2 * count - 1 - shard) * half, half)
        for t in range(4):
            outs[d][t, :half, :] = result[t, pl.ds(low, half), :]
            outs[d][t, half:, :] = result[t, pl.ds(high, half), :]


def attend(blocks, doc_ids, me):
    count = len(blocks)
    tokens = doc_ids.shape[0]
    head_size = blocks[0].shape[2]
    tiles = tokens // TILE
    longest = tokens * 5 // 8
    tile_most = min(tiles, 1 + -(-(longest - 1) // TILE))
    start = jnp.sum((doc_ids[:, None] < doc_ids[None, :]).astype(jnp.int32), axis=0)
    scalars = jnp.concatenate([me[None], start[::TILE] // TILE]).astype(jnp.int32)
    span = tile_most * TILE
    return pl.pallas_call(
        functools.partial(attention_kernel, count, tile_most),
        out_shape=[jax.ShapeDtypeStruct(b.shape, b.dtype) for b in blocks],
        in_specs=[pl.BlockSpec(memory_space=pltpu.SMEM)]
        + [pl.BlockSpec(memory_space=pltpu.VMEM)] * (count + 1),
        out_specs=[pl.BlockSpec(memory_space=pltpu.VMEM)] * count,
        scratch_shapes=[
            pltpu.VMEM((4, tokens, head_size), jnp.bfloat16),
            pltpu.VMEM((head_size, tokens), jnp.bfloat16),
            pltpu.VMEM((head_size, tokens), jnp.bfloat16),
            pltpu.VMEM((span, TILE), jnp.float32),
            pltpu.VMEM((span, TILE), jnp.bfloat16),
            pltpu.VMEM((tokens, head_size), jnp.float32),
            pltpu.VMEM((tokens, head_size), jnp.float32),
            pltpu.VMEM((4, tokens, head_size), jnp.bfloat16),
        ],
        compiler_params=pltpu.CompilerParams(vmem_limit_bytes=40 << 20),
    )(scalars, start[None, :], *blocks)


def on_device(queries, key_vecs, value_vecs, out_grad, doc_ids):
    head_count = queries.shape[1]
    count = lax.axis_size("ctx")
    me = lax.axis_index("ctx")
    copies = count // head_count

    def exchange(blocks):
        got = [blocks[0]] + [None] * (count - 1)
        for d in partner_order(count):
            got[d] = lax.ppermute(blocks[d], "ctx", [(s, s ^ d) for s in range(count)])
        return got

    arrays = (queries, key_vecs, value_vecs, out_grad)
    packed = jnp.stack([jnp.swapaxes(a, 0, 1) for a in arrays], 1)
    mine = [
        lax.dynamic_index_in_dim(packed, (me ^ d) // copies, 0, keepdims=False)
        for d in range(count)
    ]
    returned = exchange(attend(exchange(mine), doc_ids, me))
    whole = jnp.zeros_like(packed)
    for d in range(count):
        whole = lax.dynamic_update_index_in_dim(whole, returned[d], (me ^ d) // copies, 0)
    return tuple(jnp.swapaxes(whole[:, t], 0, 1) for t in range(4))


def solution(mesh):
    spec = P(("grp", "ctx"), "head", None)
    return jax.shard_map(
        on_device,
        mesh=mesh,
        in_specs=(spec, spec, spec, spec, P("grp")),
        out_specs=(spec, spec, spec, spec),
        check_vma=False,
    )
```

```python
import functools
import math

import jax
import jax.numpy as jnp
from jax import lax
from jax.experimental import pallas as pl
from jax.experimental.pallas import tpu as pltpu
from jax.sharding import PartitionSpec as P

TILE = 256
HIDDEN = -1e30


def partner_order(count):
    return sorted(range(1, count), key=lambda d: (-(d.bit_length()), -d))


def nt_dot(a, b):
    return lax.dot_general(a, b, (((1,), (1,)), ((), ())), preferred_element_type=jnp.float32)


def dot(a, b):
    return jnp.dot(a, b, preferred_element_type=jnp.float32)


def attention_kernel(count, tile_most, *refs):
    scalars, start_ref = refs[0], refs[1]
    ins = refs[2 : 2 + count]
    outs = refs[2 + count : 2 + 2 * count]
    rows, key_t, value_t, scores, weights, key_sum, value_sum, result = refs[2 + 2 * count :]
    me = scalars[0]
    shard_rows = ins[0].shape[1]
    half = shard_rows // 2
    tokens = rows.shape[1]
    head_size = rows.shape[2]
    tile = TILE
    scaling = head_size ** (-0.5)
    exponent = scaling * math.log2(math.e)

    for d in range(count):
        shard = me ^ d
        low = pl.multiple_of(shard * half, half)
        high = pl.multiple_of((2 * count - 1 - shard) * half, half)
        for t in range(4):
            rows[t, pl.ds(low, half), :] = ins[d][t, :half, :]
            rows[t, pl.ds(high, half), :] = ins[d][t, half:, :]
    for b in range(tokens // tile):
        block = pl.ds(b * tile, tile)
        key_t[:, block] = rows[1, block, :].T
        value_t[:, block] = rows[2, block, :].T
    key_sum[...] = jnp.zeros_like(key_sum)
    value_sum[...] = jnp.zeros_like(value_sum)

    def query_tile(size, j):
        q_at = pl.multiple_of(j * tile, tile)
        k_at = pl.multiple_of((j - (size - 1)) * tile, tile)
        q_blk = rows[0, pl.ds(q_at, tile), :]
        start = start_ref[:, pl.ds(q_at, tile)]
        best = jnp.full((1, tile), HIDDEN, jnp.float32)
        for i in range(size):
            s = nt_dot(rows[1, pl.ds(k_at + i * tile, tile), :], q_blk) * exponent
            k_pos = lax.broadcasted_iota(jnp.int32, (tile, tile), 0) + (k_at + i * tile)
            seen = k_pos >= start
            if i == size - 1:
                q_pos = lax.broadcasted_iota(jnp.int32, (tile, tile), 1) + q_at
                seen = seen & (k_pos <= q_pos)
            s = jnp.where(seen, s, HIDDEN)
            scores[i * tile : (i + 1) * tile, :] = s
            best = jnp.maximum(best, jnp.max(s, axis=0, keepdims=True))
        total = jnp.zeros((1, tile), jnp.float32)
        for i in range(size):
            e = jnp.exp2(scores[i * tile : (i + 1) * tile, :] - best)
            total = total + jnp.sum(e, axis=0, keepdims=True)
            weights[i * tile : (i + 1) * tile, :] = e.astype(jnp.bfloat16)
        inverse = 1.0 / total
        out_t = dot(value_t[:, pl.ds(k_at, size * tile)], weights[: size * tile, :]) * inverse
        out = out_t.astype(jnp.bfloat16)
        result[0, pl.ds(q_at, tile), :] = out_t.T.astype(jnp.bfloat16)
        grad_t = rows[3, pl.ds(q_at, tile), :].astype(jnp.float32).T * inverse
        delta = jnp.sum(grad_t * out.astype(jnp.float32), axis=0, keepdims=True)
        grad_tb = grad_t.astype(jnp.bfloat16)
        grad = grad_t.T.astype(jnp.bfloat16)
        query_t = jnp.zeros((head_size, tile), jnp.float32)
        for i in range(size):
            keys = pl.ds(k_at + i * tile, tile)
            e = weights[i * tile : (i + 1) * tile, :]
            value_sum[keys, :] += dot(e, grad)
            dprobs = dot(rows[2, keys, :], grad_tb)
            ds = (e.astype(jnp.float32) * (dprobs - delta)).astype(jnp.bfloat16)
            key_sum[keys, :] += dot(ds, q_blk)
            query_t = query_t + dot(key_t[:, keys], ds)
        result[1, pl.ds(q_at, tile), :] = (query_t * scaling).T.astype(jnp.bfloat16)

    @pl.loop(0, tokens // tile)
    def _(j):
        size = j - scalars[1 + j] + 1
        for n in range(1, tile_most + 1):

            @pl.when(size == n)
            def _(n=n):
                query_tile(n, j)

    result[2] = (key_sum[...] * scaling).astype(jnp.bfloat16)
    result[3] = value_sum[...].astype(jnp.bfloat16)
    for d in range(count):
        shard = me ^ d
        low = pl.multiple_of(shard * half, half)
        high = pl.multiple_of((2 * count - 1 - shard) * half, half)
        for t in range(4):
            outs[d][t, :half, :] = result[t, pl.ds(low, half), :]
            outs[d][t, half:, :] = result[t, pl.ds(high, half), :]


def attend(blocks, doc_ids, me):
    count = len(blocks)
    tokens = doc_ids.shape[0]
    head_size = blocks[0].shape[2]
    tiles = tokens // TILE
    longest = tokens * 5 // 8
    tile_most = min(tiles, 1 + -(-(longest - 1) // TILE))
    start = jnp.sum((doc_ids[:, None] < doc_ids[None, :]).astype(jnp.int32), axis=0)
    scalars = jnp.concatenate([me[None], start[::TILE] // TILE]).astype(jnp.int32)
    span = tile_most * TILE
    return pl.pallas_call(
        functools.partial(attention_kernel, count, tile_most),
        out_shape=[jax.ShapeDtypeStruct(b.shape, b.dtype) for b in blocks],
        in_specs=[pl.BlockSpec(memory_space=pltpu.SMEM)]
        + [pl.BlockSpec(memory_space=pltpu.VMEM)] * (count + 1),
        out_specs=[pl.BlockSpec(memory_space=pltpu.VMEM)] * count,
        scratch_shapes=[
            pltpu.VMEM((4, tokens, head_size), jnp.bfloat16),
            pltpu.VMEM((head_size, tokens), jnp.bfloat16),
            pltpu.VMEM((head_size, tokens), jnp.bfloat16),
            pltpu.VMEM((span, TILE), jnp.float32),
            pltpu.VMEM((span, TILE), jnp.bfloat16),
            pltpu.VMEM((tokens, head_size), jnp.float32),
            pltpu.VMEM((tokens, head_size), jnp.float32),
            pltpu.VMEM((4, tokens, head_size), jnp.bfloat16),
        ],
        compiler_params=pltpu.CompilerParams(vmem_limit_bytes=40 << 20),
    )(scalars, start[None, :], *blocks)


def unpack_kernel(count, copies, *refs):
    scalars = refs[0]
    ins = refs[1 : 1 + count]
    outs = refs[1 + count : 5 + count]
    heads, turned, done = refs[5 + count :]
    me = scalars[0]
    sends = []
    for t in range(4):
        for d in range(count):
            heads[t, (me ^ d) // copies] = ins[d][t]
        turned[t] = jnp.swapaxes(heads[t], 0, 1)
        send = pltpu.make_async_copy(turned.at[t], outs[t], done.at[t])
        send.start()
        sends.append(send)
    for send in sends:
        send.wait()


def unpack(blocks, me, head_count):
    count = len(blocks)
    kinds, shard_rows, head_size = blocks[0].shape
    shape = (shard_rows, head_count, head_size)
    return pl.pallas_call(
        functools.partial(unpack_kernel, count, count // head_count),
        out_shape=[jax.ShapeDtypeStruct(shape, blocks[0].dtype)] * kinds,
        in_specs=[pl.BlockSpec(memory_space=pltpu.SMEM)]
        + [pl.BlockSpec(memory_space=pltpu.VMEM)] * count,
        out_specs=[pl.BlockSpec(memory_space=pl.ANY)] * kinds,
        scratch_shapes=[
            pltpu.VMEM((kinds, head_count, shard_rows, head_size), blocks[0].dtype),
            pltpu.VMEM((kinds,) + shape, blocks[0].dtype),
            pltpu.SemaphoreType.DMA((kinds,)),
        ],
        compiler_params=pltpu.CompilerParams(vmem_limit_bytes=40 << 20),
    )(me[None].astype(jnp.int32), *blocks)


def on_device(queries, key_vecs, value_vecs, out_grad, doc_ids):
    head_count = queries.shape[1]
    count = lax.axis_size("ctx")
    me = lax.axis_index("ctx")
    copies = count // head_count

    def exchange(blocks):
        got = [blocks[0]] + [None] * (count - 1)
        for d in partner_order(count):
            got[d] = lax.ppermute(blocks[d], "ctx", [(s, s ^ d) for s in range(count)])
        return got

    arrays = (queries, key_vecs, value_vecs, out_grad)
    packed = jnp.stack([jnp.swapaxes(a, 0, 1) for a in arrays], 1)
    mine = [
        lax.dynamic_index_in_dim(packed, (me ^ d) // copies, 0, keepdims=False)
        for d in range(count)
    ]
    returned = exchange(attend(exchange(mine), doc_ids, me))
    return tuple(unpack(returned, me, head_count))


def solution(mesh):
    spec = P(("grp", "ctx"), "head", None)
    return jax.shard_map(
        on_device,
        mesh=mesh,
        in_specs=(spec, spec, spec, spec, P("grp")),
        out_specs=(spec, spec, spec, spec),
        check_vma=False,
    )
```

```python
import functools
import math

import jax
import jax.numpy as jnp
from jax import lax
from jax.experimental import pallas as pl
from jax.experimental.pallas import tpu as pltpu
from jax.sharding import PartitionSpec as P

TILE = 256
HIDDEN = -1e30


def partner_orders(count):
    far, near = list(range(count - 1, count // 2 - 1, -1)), list(range(count // 2 - 1, 0, -1))
    return (0, *far[:1], *near, *far[1:]), (0, *far[1:], *far[:1], *near)


def nt_dot(a, b):
    return lax.dot_general(a, b, (((1,), (1,)), ((), ())), preferred_element_type=jnp.float32)


def dot(a, b):
    return jnp.dot(a, b, preferred_element_type=jnp.float32)


def attention_kernel(order, tile_most, *refs):
    count = len(order)
    scalars, start_ref = refs[0], refs[1]
    ins = refs[2 : 2 + count]
    outs = refs[2 + count : 2 + 2 * count]
    rows, key_t, value_t, scores, weights, key_sum, value_sum, result = refs[2 + 2 * count :]
    me = scalars[0]
    shard_rows = ins[0].shape[1]
    half = shard_rows // 2
    tokens = rows.shape[1]
    head_size = rows.shape[2]
    tile = TILE
    scaling = head_size ** (-0.5)
    exponent = scaling * math.log2(math.e)

    for n, d in enumerate(order):
        shard = me ^ d
        low = pl.multiple_of(shard * half, half)
        high = pl.multiple_of((2 * count - 1 - shard) * half, half)
        for t in range(4):
            rows[t, pl.ds(low, half), :] = ins[n][t, :half, :]
            rows[t, pl.ds(high, half), :] = ins[n][t, half:, :]
    for b in range(tokens // tile):
        block = pl.ds(b * tile, tile)
        key_t[:, block] = rows[1, block, :].T
        value_t[:, block] = rows[2, block, :].T
    key_sum[...] = jnp.zeros_like(key_sum)
    value_sum[...] = jnp.zeros_like(value_sum)

    def query_tile(size, j):
        q_at = pl.multiple_of(j * tile, tile)
        k_at = pl.multiple_of((j - (size - 1)) * tile, tile)
        q_blk = rows[0, pl.ds(q_at, tile), :]
        start = start_ref[:, pl.ds(q_at, tile)]
        best = jnp.full((1, tile), HIDDEN, jnp.float32)
        for i in range(size):
            s = nt_dot(rows[1, pl.ds(k_at + i * tile, tile), :], q_blk) * exponent
            k_pos = lax.broadcasted_iota(jnp.int32, (tile, tile), 0) + (k_at + i * tile)
            seen = k_pos >= start
            if i == size - 1:
                q_pos = lax.broadcasted_iota(jnp.int32, (tile, tile), 1) + q_at
                seen = seen & (k_pos <= q_pos)
            s = jnp.where(seen, s, HIDDEN)
            scores[i * tile : (i + 1) * tile, :] = s
            best = jnp.maximum(best, jnp.max(s, axis=0, keepdims=True))
        total = jnp.zeros((1, tile), jnp.float32)
        for i in range(size):
            e = jnp.exp2(scores[i * tile : (i + 1) * tile, :] - best)
            total = total + jnp.sum(e, axis=0, keepdims=True)
            weights[i * tile : (i + 1) * tile, :] = e.astype(jnp.bfloat16)
        inverse = 1.0 / total
        out_t = dot(value_t[:, pl.ds(k_at, size * tile)], weights[: size * tile, :]) * inverse
        out = out_t.astype(jnp.bfloat16)
        result[0, pl.ds(q_at, tile), :] = out_t.T.astype(jnp.bfloat16)
        grad_t = rows[3, pl.ds(q_at, tile), :].astype(jnp.float32).T * inverse
        delta = jnp.sum(grad_t * out.astype(jnp.float32), axis=0, keepdims=True)
        grad_tb = grad_t.astype(jnp.bfloat16)
        grad = grad_t.T.astype(jnp.bfloat16)
        query_t = jnp.zeros((head_size, tile), jnp.float32)
        for i in range(size):
            keys = pl.ds(k_at + i * tile, tile)
            e = weights[i * tile : (i + 1) * tile, :]
            value_sum[keys, :] += dot(e, grad)
            dprobs = dot(rows[2, keys, :], grad_tb)
            ds = (e.astype(jnp.float32) * (dprobs - delta)).astype(jnp.bfloat16)
            key_sum[keys, :] += dot(ds, q_blk)
            query_t = query_t + dot(key_t[:, keys], ds)
        result[1, pl.ds(q_at, tile), :] = (query_t * scaling).T.astype(jnp.bfloat16)

    @pl.loop(0, tokens // tile)
    def _(j):
        size = j - scalars[1 + j] + 1
        for n in range(1, tile_most + 1):

            @pl.when(size == n)
            def _(n=n):
                query_tile(n, j)

    result[2] = (key_sum[...] * scaling).astype(jnp.bfloat16)
    result[3] = value_sum[...].astype(jnp.bfloat16)
    for n, d in enumerate(order):
        shard = me ^ d
        low = pl.multiple_of(shard * half, half)
        high = pl.multiple_of((2 * count - 1 - shard) * half, half)
        for t in range(4):
            outs[n][t, :half, :] = result[t, pl.ds(low, half), :]
            outs[n][t, half:, :] = result[t, pl.ds(high, half), :]


def attend(blocks, order, doc_ids, me):
    count = len(blocks)
    tokens = doc_ids.shape[0]
    head_size = blocks[0].shape[2]
    tiles = tokens // TILE
    longest = tokens * 5 // 8
    tile_most = min(tiles, 1 + -(-(longest - 1) // TILE))
    start = jnp.sum((doc_ids[:, None] < doc_ids[None, :]).astype(jnp.int32), axis=0)
    scalars = jnp.concatenate([me[None], start[::TILE] // TILE]).astype(jnp.int32)
    span = tile_most * TILE
    return pl.pallas_call(
        functools.partial(attention_kernel, order, tile_most),
        out_shape=[jax.ShapeDtypeStruct(b.shape, b.dtype) for b in blocks],
        in_specs=[pl.BlockSpec(memory_space=pltpu.SMEM)]
        + [pl.BlockSpec(memory_space=pltpu.VMEM)] * (count + 1),
        out_specs=[pl.BlockSpec(memory_space=pltpu.VMEM)] * count,
        scratch_shapes=[
            pltpu.VMEM((4, tokens, head_size), jnp.bfloat16),
            pltpu.VMEM((head_size, tokens), jnp.bfloat16),
            pltpu.VMEM((head_size, tokens), jnp.bfloat16),
            pltpu.VMEM((span, TILE), jnp.float32),
            pltpu.VMEM((span, TILE), jnp.bfloat16),
            pltpu.VMEM((tokens, head_size), jnp.float32),
            pltpu.VMEM((tokens, head_size), jnp.float32),
            pltpu.VMEM((4, tokens, head_size), jnp.bfloat16),
        ],
        compiler_params=pltpu.CompilerParams(vmem_limit_bytes=40 << 20),
    )(scalars, start[None, :], *blocks)


def pack_kernel(order, copies, *refs):
    count = len(order)
    scalars = refs[0]
    ins = refs[1:5]
    outs = refs[5 : 5 + count]
    held, heads, done = refs[5 + count :]
    me = scalars[0]
    loads = [pltpu.make_async_copy(ins[t], held.at[t], done.at[t]) for t in range(4)]
    for load in loads:
        load.start()
    for t in range(4):
        loads[t].wait()
        heads[t] = jnp.swapaxes(held[t], 0, 1)
        for n, d in enumerate(order):
            outs[n][t] = heads[t, (me ^ d) // copies]


def pack(arrays, order, me):
    count = len(order)
    shard_rows, head_count, head_size = arrays[0].shape
    kinds = len(arrays)
    return pl.pallas_call(
        functools.partial(pack_kernel, order, count // head_count),
        out_shape=[jax.ShapeDtypeStruct((kinds, shard_rows, head_size), arrays[0].dtype)] * count,
        in_specs=[pl.BlockSpec(memory_space=pltpu.SMEM)]
        + [pl.BlockSpec(memory_space=pltpu.HBM)] * kinds,
        out_specs=[pl.BlockSpec(memory_space=pltpu.VMEM)] * count,
        scratch_shapes=[
            pltpu.VMEM((kinds,) + arrays[0].shape, arrays[0].dtype),
            pltpu.VMEM((kinds, head_count, shard_rows, head_size), arrays[0].dtype),
            pltpu.SemaphoreType.DMA((kinds,)),
        ],
        compiler_params=pltpu.CompilerParams(vmem_limit_bytes=40 << 20),
    )(me[None].astype(jnp.int32), *[pltpu.with_memory_space_constraint(a, pltpu.HBM) for a in arrays])


def unpack_kernel(order, copies, *refs):
    count = len(order)
    scalars = refs[0]
    ins = refs[1 : 1 + count]
    outs = refs[1 + count : 5 + count]
    heads, turned, done = refs[5 + count :]
    me = scalars[0]
    sends = []
    for t in range(4):
        for n, d in enumerate(order):
            heads[t, (me ^ d) // copies] = ins[n][t]
        turned[t] = jnp.swapaxes(heads[t], 0, 1)
        send = pltpu.make_async_copy(turned.at[t], outs[t], done.at[t])
        send.start()
        sends.append(send)
    for send in sends:
        send.wait()


def unpack(blocks, order, me, head_count):
    count = len(blocks)
    kinds, shard_rows, head_size = blocks[0].shape
    shape = (shard_rows, head_count, head_size)
    return pl.pallas_call(
        functools.partial(unpack_kernel, order, count // head_count),
        out_shape=[jax.ShapeDtypeStruct(shape, blocks[0].dtype)] * kinds,
        in_specs=[pl.BlockSpec(memory_space=pltpu.SMEM)]
        + [pl.BlockSpec(memory_space=pltpu.VMEM)] * count,
        out_specs=[pl.BlockSpec(memory_space=pltpu.HBM)] * kinds,
        scratch_shapes=[
            pltpu.VMEM((kinds, head_count, shard_rows, head_size), blocks[0].dtype),
            pltpu.VMEM((kinds,) + shape, blocks[0].dtype),
            pltpu.SemaphoreType.DMA((kinds,)),
        ],
        compiler_params=pltpu.CompilerParams(vmem_limit_bytes=40 << 20),
    )(me[None].astype(jnp.int32), *blocks)


def on_device(queries, key_vecs, value_vecs, out_grad, doc_ids):
    head_count = queries.shape[1]
    count = lax.axis_size("ctx")
    me = lax.axis_index("ctx")
    order, back = partner_orders(count)

    def exchange(blocks, order):
        got = {0: blocks[0]}
        for d in order[1:]:
            got[d] = lax.ppermute(blocks[d], "ctx", [(s, s ^ d) for s in range(count)])
        return got

    arrays = (queries, key_vecs, value_vecs, out_grad)
    mine = dict(zip(order, pack(arrays, order, me)))
    got = exchange(mine, order)
    results = attend([got[d] for d in order], order, doc_ids, me)
    returned = exchange(dict(zip(order, results)), back)
    return tuple(unpack([returned[d] for d in back], back, me, head_count))


def solution(mesh):
    spec = P(("grp", "ctx"), "head", None)
    return jax.shard_map(
        on_device,
        mesh=mesh,
        in_specs=(spec, spec, spec, spec, P("grp")),
        out_specs=(spec, spec, spec, spec),
        check_vma=False,
    )
```

```python
import functools
import math

import jax
import jax.numpy as jnp
from jax import lax
from jax.experimental import pallas as pl
from jax.experimental.pallas import tpu as pltpu
from jax.sharding import PartitionSpec as P

TILE = 256
HIDDEN = -1e30


def partner_orders(count):
    far, near = list(range(count - 1, count // 2 - 1, -1)), list(range(count // 2 - 1, 0, -1))
    turns = [d for pair in zip(far, near) for d in pair] + far[-1:]
    back = near + far
    return (0, *turns), (0, *back[count // 2 :], *back[: count // 2])


def nt_dot(a, b):
    return lax.dot_general(a, b, (((1,), (1,)), ((), ())), preferred_element_type=jnp.float32)


def dot(a, b):
    return jnp.dot(a, b, preferred_element_type=jnp.float32)


def attention_kernel(order, tile_most, *refs):
    count = len(order)
    scalars, start_ref = refs[0], refs[1]
    ins = refs[2 : 2 + count]
    outs = refs[2 + count : 2 + 2 * count]
    rows, key_t, value_t, scores, weights, dweights, key_sum, value_sum, result = refs[2 + 2 * count :]
    me = scalars[0]
    shard_rows = ins[0].shape[1]
    half = shard_rows // 2
    tokens = rows.shape[1]
    head_size = rows.shape[2]
    tile = TILE
    scaling = head_size ** (-0.5)
    exponent = scaling * math.log2(math.e)

    for n, d in enumerate(order):
        shard = me ^ d
        low = pl.multiple_of(shard * half, half)
        high = pl.multiple_of((2 * count - 1 - shard) * half, half)
        for t in range(4):
            rows[t, pl.ds(low, half), :] = ins[n][t, :half, :]
            rows[t, pl.ds(high, half), :] = ins[n][t, half:, :]
    for b in range(tokens // tile):
        block = pl.ds(b * tile, tile)
        key_t[:, block] = rows[1, block, :].T
        value_t[:, block] = rows[2, block, :].T
    key_sum[...] = jnp.zeros_like(key_sum)
    value_sum[...] = jnp.zeros_like(value_sum)

    wide = 2 * tile

    def query_tile(size, j):
        q_at = j * wide
        k_at = q_at + wide - size * tile
        q_blk = rows[0, pl.ds(q_at, wide), :]
        start = start_ref[:, pl.ds(q_at, wide)]
        query_tb = q_blk.T

        def cols(i):
            return slice(tile, wide) if i == size - 1 else slice(0, wide)

        best = jnp.full((1, wide), HIDDEN, jnp.float32)
        for i in range(size):
            c = cols(i)
            n = c.stop - c.start
            s = dot(rows[1, pl.ds(k_at + i * tile, tile), :], query_tb[:, c]) * exponent
            k_pos = lax.broadcasted_iota(jnp.int32, (tile, n), 0) + (k_at + i * tile)
            seen = k_pos >= start[:, c]
            if i >= size - 2:
                q_pos = lax.broadcasted_iota(jnp.int32, (tile, n), 1) + (q_at + c.start)
                seen = seen & (k_pos <= q_pos)
            s = jnp.where(seen, s, HIDDEN)
            scores[i * tile : (i + 1) * tile, c] = s
            top = jnp.max(s, axis=0, keepdims=True)
            if i == size - 1:
                best = jnp.concatenate([best[:, :tile], jnp.maximum(best[:, tile:], top)], 1)
            else:
                best = jnp.maximum(best, top)
        total = jnp.zeros((1, wide), jnp.float32)
        for i in range(size):
            c = cols(i)
            e = jnp.exp2(scores[i * tile : (i + 1) * tile, c] - best[:, c])
            part = jnp.sum(e, axis=0, keepdims=True)
            if i == size - 1:
                total = jnp.concatenate([total[:, :tile], total[:, tile:] + part], 1)
            else:
                total = total + part
            weights[i * tile : (i + 1) * tile, c] = e.astype(jnp.bfloat16)
        inverse = 1.0 / total
        body = size - 1
        out_t = dot(value_t[:, pl.ds(k_at, body * tile)], weights[: body * tile, :])
        last = dot(value_t[:, pl.ds(k_at + body * tile, tile)], weights[body * tile : size * tile, tile:])
        out_t = jnp.concatenate([out_t[:, :tile], out_t[:, tile:] + last], 1) * inverse
        out = out_t.astype(jnp.bfloat16)
        result[0, pl.ds(q_at, wide), :] = out_t.T.astype(jnp.bfloat16)
        grad_t = rows[3, pl.ds(q_at, wide), :].astype(jnp.float32).T * inverse
        delta = jnp.sum(grad_t * out.astype(jnp.float32), axis=0, keepdims=True)
        grad_tb = grad_t.astype(jnp.bfloat16)
        for i in range(size):
            c = cols(i)
            keys = pl.ds(k_at + i * tile, tile)
            e = weights[i * tile : (i + 1) * tile, c]
            value_sum[:, keys] += nt_dot(grad_tb[:, c], e)
            dprobs = dot(rows[2, keys, :], grad_tb[:, c])
            ds = (e.astype(jnp.float32) * (dprobs - delta[:, c])).astype(jnp.bfloat16)
            dweights[i * tile : (i + 1) * tile, c] = ds
        for i in range(size):
            c = cols(i)
            keys = pl.ds(k_at + i * tile, tile)
            key_sum[:, keys] += nt_dot(query_tb[:, c], dweights[i * tile : (i + 1) * tile, c])
        query_t = dot(key_t[:, pl.ds(k_at, body * tile)], dweights[: body * tile, :])
        last = dot(key_t[:, pl.ds(k_at + body * tile, tile)], dweights[body * tile : size * tile, tile:])
        query_t = jnp.concatenate([query_t[:, :tile], query_t[:, tile:] + last], 1)
        result[1, pl.ds(q_at, wide), :] = (query_t * scaling).T.astype(jnp.bfloat16)

    for j in range(tokens // wide):
        query_tile(min(2 * j + 2, tile_most), j)

    for b in range(tokens // tile):
        block = pl.ds(b * tile, tile)
        result[2, block, :] = (key_sum[:, block] * scaling).T.astype(jnp.bfloat16)
        result[3, block, :] = value_sum[:, block].T.astype(jnp.bfloat16)
    for n, d in enumerate(order):
        shard = me ^ d
        low = pl.multiple_of(shard * half, half)
        high = pl.multiple_of((2 * count - 1 - shard) * half, half)
        for t in range(4):
            outs[n][t, :half, :] = result[t, pl.ds(low, half), :]
            outs[n][t, half:, :] = result[t, pl.ds(high, half), :]


def attend(blocks, order, doc_ids, me):
    count = len(blocks)
    tokens = doc_ids.shape[0]
    head_size = blocks[0].shape[2]
    tiles = tokens // TILE
    longest = tokens * 5 // 8
    tile_most = min(tiles, 2 + -(-(longest - 1) // TILE))
    start = jnp.sum((doc_ids[:, None] < doc_ids[None, :]).astype(jnp.int32), axis=0)
    scalars = me[None].astype(jnp.int32)
    span = tile_most * TILE
    return pl.pallas_call(
        functools.partial(attention_kernel, order, tile_most),
        out_shape=[jax.ShapeDtypeStruct(b.shape, b.dtype) for b in blocks],
        in_specs=[pl.BlockSpec(memory_space=pltpu.SMEM)]
        + [pl.BlockSpec(memory_space=pltpu.VMEM)] * (count + 1),
        out_specs=[pl.BlockSpec(memory_space=pltpu.VMEM)] * count,
        scratch_shapes=[
            pltpu.VMEM((4, tokens, head_size), jnp.bfloat16),
            pltpu.VMEM((head_size, tokens), jnp.bfloat16),
            pltpu.VMEM((head_size, tokens), jnp.bfloat16),
            pltpu.VMEM((span, 2 * TILE), jnp.float32),
            pltpu.VMEM((span, 2 * TILE), jnp.bfloat16),
            pltpu.VMEM((span, 2 * TILE), jnp.bfloat16),
            pltpu.VMEM((head_size, tokens), jnp.float32),
            pltpu.VMEM((head_size, tokens), jnp.float32),
            pltpu.VMEM((4, tokens, head_size), jnp.bfloat16),
        ],
        compiler_params=pltpu.CompilerParams(vmem_limit_bytes=40 << 20),
    )(scalars, start[None, :], *blocks)


def pack_kernel(order, copies, *refs):
    count = len(order)
    scalars = refs[0]
    ins = refs[1:5]
    outs = refs[5 : 5 + count]
    held, heads, done = refs[5 + count :]
    me = scalars[0]
    loads = [pltpu.make_async_copy(ins[t], held.at[t], done.at[t]) for t in range(4)]
    for load in loads:
        load.start()
    for t in range(4):
        loads[t].wait()
        heads[t] = jnp.swapaxes(held[t], 0, 1)
        for n, d in enumerate(order):
            outs[n][t] = heads[t, (me ^ d) // copies]


def pack(arrays, order, me):
    count = len(order)
    shard_rows, head_count, head_size = arrays[0].shape
    kinds = len(arrays)
    return pl.pallas_call(
        functools.partial(pack_kernel, order, count // head_count),
        out_shape=[jax.ShapeDtypeStruct((kinds, shard_rows, head_size), arrays[0].dtype)] * count,
        in_specs=[pl.BlockSpec(memory_space=pltpu.SMEM)]
        + [pl.BlockSpec(memory_space=pltpu.HBM)] * kinds,
        out_specs=[pl.BlockSpec(memory_space=pltpu.VMEM)] * count,
        scratch_shapes=[
            pltpu.VMEM((kinds,) + arrays[0].shape, arrays[0].dtype),
            pltpu.VMEM((kinds, head_count, shard_rows, head_size), arrays[0].dtype),
            pltpu.SemaphoreType.DMA((kinds,)),
        ],
        compiler_params=pltpu.CompilerParams(vmem_limit_bytes=40 << 20),
    )(me[None].astype(jnp.int32), *[pltpu.with_memory_space_constraint(a, pltpu.HBM) for a in arrays])


def unpack_kernel(order, copies, *refs):
    count = len(order)
    scalars = refs[0]
    ins = refs[1 : 1 + count]
    outs = refs[1 + count : 5 + count]
    heads, turned, done = refs[5 + count :]
    me = scalars[0]
    sends = []
    for t in range(4):
        for n, d in enumerate(order):
            heads[t, (me ^ d) // copies] = ins[n][t]
        turned[t] = jnp.swapaxes(heads[t], 0, 1)
        send = pltpu.make_async_copy(turned.at[t], outs[t], done.at[t])
        send.start()
        sends.append(send)
    for send in sends:
        send.wait()


def unpack(blocks, order, me, head_count):
    count = len(blocks)
    kinds, shard_rows, head_size = blocks[0].shape
    shape = (shard_rows, head_count, head_size)
    return pl.pallas_call(
        functools.partial(unpack_kernel, order, count // head_count),
        out_shape=[jax.ShapeDtypeStruct(shape, blocks[0].dtype)] * kinds,
        in_specs=[pl.BlockSpec(memory_space=pltpu.SMEM)]
        + [pl.BlockSpec(memory_space=pltpu.VMEM)] * count,
        out_specs=[pl.BlockSpec(memory_space=pltpu.HBM)] * kinds,
        scratch_shapes=[
            pltpu.VMEM((kinds, head_count, shard_rows, head_size), blocks[0].dtype),
            pltpu.VMEM((kinds,) + shape, blocks[0].dtype),
            pltpu.SemaphoreType.DMA((kinds,)),
        ],
        compiler_params=pltpu.CompilerParams(vmem_limit_bytes=40 << 20),
    )(me[None].astype(jnp.int32), *blocks)


def on_device(queries, key_vecs, value_vecs, out_grad, doc_ids):
    head_count = queries.shape[1]
    count = lax.axis_size("ctx")
    me = lax.axis_index("ctx")
    order, back = partner_orders(count)

    def exchange(blocks, order):
        got = {0: blocks[0]}
        for d in order[1:]:
            got[d] = lax.ppermute(blocks[d], "ctx", [(s, s ^ d) for s in range(count)])
        return got

    arrays = (queries, key_vecs, value_vecs, out_grad)
    mine = dict(zip(order, pack(arrays, order, me)))
    got = exchange(mine, order)
    results = attend([got[d] for d in order], order, doc_ids, me)
    returned = exchange(dict(zip(order, results)), back)
    return tuple(unpack([returned[d] for d in back], back, me, head_count))


def solution(mesh):
    spec = P(("grp", "ctx"), "head", None)
    return jax.shard_map(
        on_device,
        mesh=mesh,
        in_specs=(spec, spec, spec, spec, P("grp")),
        out_specs=(spec, spec, spec, spec),
        check_vma=False,
    )
```

```python
import functools
import math

import jax
import jax.numpy as jnp
from jax import lax
from jax.experimental import pallas as pl
from jax.experimental.pallas import tpu as pltpu
from jax.sharding import PartitionSpec as P

TILE = 256
HIDDEN = -1e30


def partner_orders(count):
    far, near = list(range(count - 1, count // 2 - 1, -1)), list(range(count // 2 - 1, 0, -1))
    first = far[count // 4 :] + far[: count // 4]
    turns = [d for pair in zip(first, near) for d in pair] + first[-1:]
    back = near + far
    return (0, *turns), (0, *back[count // 2 :], *back[: count // 2])


def nt_dot(a, b):
    return lax.dot_general(a, b, (((1,), (1,)), ((), ())), preferred_element_type=jnp.float32)


def dot(a, b):
    return jnp.dot(a, b, preferred_element_type=jnp.float32)


def attention_kernel(order, tile_most, *refs):
    count = len(order)
    scalars, start_ref = refs[0], refs[1]
    ins = refs[2 : 2 + count]
    outs = refs[2 + count : 2 + 2 * count]
    rows, key_t, value_t, scores, weights, dweights, key_sum, value_sum, result = refs[2 + 2 * count :]
    me = scalars[0]
    shard_rows = ins[0].shape[1]
    half = shard_rows // 2
    tokens = rows.shape[1]
    head_size = rows.shape[2]
    tile = TILE
    scaling = head_size ** (-0.5)
    exponent = scaling * math.log2(math.e)

    for n, d in enumerate(order):
        shard = me ^ d
        low = pl.multiple_of(shard * half, half)
        high = pl.multiple_of((2 * count - 1 - shard) * half, half)
        for t in range(4):
            rows[t, pl.ds(low, half), :] = ins[n][t, :half, :]
            rows[t, pl.ds(high, half), :] = ins[n][t, half:, :]
    for b in range(tokens // tile):
        block = pl.ds(b * tile, tile)
        key_t[:, block] = rows[1, block, :].T
        value_t[:, block] = rows[2, block, :].T
    key_sum[...] = jnp.zeros_like(key_sum)
    value_sum[...] = jnp.zeros_like(value_sum)

    wide = 2 * tile

    def query_tile(size, j):
        q_at = j * wide
        k_at = q_at + wide - size * tile
        q_blk = rows[0, pl.ds(q_at, wide), :]
        start = start_ref[:, pl.ds(q_at, wide)]
        query_tb = q_blk.T

        def cols(i):
            return slice(tile, wide) if i == size - 1 else slice(0, wide)

        best = jnp.full((1, wide), HIDDEN, jnp.float32)
        for i in range(size):
            c = cols(i)
            n = c.stop - c.start
            s = dot(rows[1, pl.ds(k_at + i * tile, tile), :], query_tb[:, c]) * exponent
            k_pos = lax.broadcasted_iota(jnp.int32, (tile, n), 0) + (k_at + i * tile)
            seen = k_pos >= start[:, c]
            if i >= size - 2:
                q_pos = lax.broadcasted_iota(jnp.int32, (tile, n), 1) + (q_at + c.start)
                seen = seen & (k_pos <= q_pos)
            s = jnp.where(seen, s, HIDDEN)
            scores[i * tile : (i + 1) * tile, c] = s
            top = jnp.max(s, axis=0, keepdims=True)
            if i == size - 1:
                best = jnp.concatenate([best[:, :tile], jnp.maximum(best[:, tile:], top)], 1)
            else:
                best = jnp.maximum(best, top)
        total = jnp.zeros((1, wide), jnp.float32)
        for i in range(size):
            c = cols(i)
            e = jnp.exp2(scores[i * tile : (i + 1) * tile, c] - best[:, c])
            part = jnp.sum(e, axis=0, keepdims=True)
            if i == size - 1:
                total = jnp.concatenate([total[:, :tile], total[:, tile:] + part], 1)
            else:
                total = total + part
            weights[i * tile : (i + 1) * tile, c] = e.astype(jnp.bfloat16)
        inverse = 1.0 / total
        body = size - 1
        out_t = dot(value_t[:, pl.ds(k_at, body * tile)], weights[: body * tile, :])
        last = dot(value_t[:, pl.ds(k_at + body * tile, tile)], weights[body * tile : size * tile, tile:])
        out_t = jnp.concatenate([out_t[:, :tile], out_t[:, tile:] + last], 1) * inverse
        out = out_t.astype(jnp.bfloat16)
        result[0, pl.ds(q_at, wide), :] = out_t.T.astype(jnp.bfloat16)
        grad_t = rows[3, pl.ds(q_at, wide), :].astype(jnp.float32).T * inverse
        delta = jnp.sum(grad_t * out.astype(jnp.float32), axis=0, keepdims=True)
        grad_tb = grad_t.astype(jnp.bfloat16)
        for i in range(size):
            c = cols(i)
            keys = pl.ds(k_at + i * tile, tile)
            e = weights[i * tile : (i + 1) * tile, c]
            value_sum[:, keys] += nt_dot(grad_tb[:, c], e)
            dprobs = dot(rows[2, keys, :], grad_tb[:, c])
            ds = (e.astype(jnp.float32) * (dprobs - delta[:, c])).astype(jnp.bfloat16)
            dweights[i * tile : (i + 1) * tile, c] = ds
        for i in range(size):
            c = cols(i)
            keys = pl.ds(k_at + i * tile, tile)
            key_sum[:, keys] += nt_dot(query_tb[:, c], dweights[i * tile : (i + 1) * tile, c])
        query_t = dot(key_t[:, pl.ds(k_at, body * tile)], dweights[: body * tile, :])
        last = dot(key_t[:, pl.ds(k_at + body * tile, tile)], dweights[body * tile : size * tile, tile:])
        query_t = jnp.concatenate([query_t[:, :tile], query_t[:, tile:] + last], 1)
        result[1, pl.ds(q_at, wide), :] = (query_t * scaling).T.astype(jnp.bfloat16)

    for j in range(tokens // wide):
        query_tile(min(2 * j + 2, tile_most), j)

    for b in range(tokens // tile):
        block = pl.ds(b * tile, tile)
        result[2, block, :] = (key_sum[:, block] * scaling).T.astype(jnp.bfloat16)
        result[3, block, :] = value_sum[:, block].T.astype(jnp.bfloat16)
    for n, d in enumerate(order):
        shard = me ^ d
        low = pl.multiple_of(shard * half, half)
        high = pl.multiple_of((2 * count - 1 - shard) * half, half)
        for t in range(4):
            outs[n][t, :half, :] = result[t, pl.ds(low, half), :]
            outs[n][t, half:, :] = result[t, pl.ds(high, half), :]


def attend(blocks, order, doc_ids, me):
    count = len(blocks)
    tokens = doc_ids.shape[0]
    head_size = blocks[0].shape[2]
    tiles = tokens // TILE
    longest = tokens * 5 // 8
    tile_most = min(tiles, 2 + -(-(longest - 1) // TILE))
    start = jnp.sum((doc_ids[:, None] < doc_ids[None, :]).astype(jnp.int32), axis=0)
    scalars = me[None].astype(jnp.int32)
    span = tile_most * TILE
    return pl.pallas_call(
        functools.partial(attention_kernel, order, tile_most),
        out_shape=[jax.ShapeDtypeStruct(b.shape, b.dtype) for b in blocks],
        in_specs=[pl.BlockSpec(memory_space=pltpu.SMEM)]
        + [pl.BlockSpec(memory_space=pltpu.VMEM)] * (count + 1),
        out_specs=[pl.BlockSpec(memory_space=pltpu.VMEM)] * count,
        scratch_shapes=[
            pltpu.VMEM((4, tokens, head_size), jnp.bfloat16),
            pltpu.VMEM((head_size, tokens), jnp.bfloat16),
            pltpu.VMEM((head_size, tokens), jnp.bfloat16),
            pltpu.VMEM((span, 2 * TILE), jnp.float32),
            pltpu.VMEM((span, 2 * TILE), jnp.bfloat16),
            pltpu.VMEM((span, 2 * TILE), jnp.bfloat16),
            pltpu.VMEM((head_size, tokens), jnp.float32),
            pltpu.VMEM((head_size, tokens), jnp.float32),
            pltpu.VMEM((4, tokens, head_size), jnp.bfloat16),
        ],
        compiler_params=pltpu.CompilerParams(vmem_limit_bytes=40 << 20),
    )(scalars, start[None, :], *blocks)


def pack_kernel(order, copies, *refs):
    count = len(order)
    scalars = refs[0]
    ins = refs[1:5]
    outs = refs[5 : 5 + count]
    held, heads, done = refs[5 + count :]
    me = scalars[0]
    loads = [pltpu.make_async_copy(ins[t], held.at[t], done.at[t]) for t in range(4)]
    for load in loads:
        load.start()
    for t in range(4):
        loads[t].wait()
        heads[t] = jnp.swapaxes(held[t], 0, 1)
        for n, d in enumerate(order):
            outs[n][t] = heads[t, (me ^ d) // copies]


def pack(arrays, order, me):
    count = len(order)
    shard_rows, head_count, head_size = arrays[0].shape
    kinds = len(arrays)
    return pl.pallas_call(
        functools.partial(pack_kernel, order, count // head_count),
        out_shape=[jax.ShapeDtypeStruct((kinds, shard_rows, head_size), arrays[0].dtype)] * count,
        in_specs=[pl.BlockSpec(memory_space=pltpu.SMEM)]
        + [pl.BlockSpec(memory_space=pltpu.HBM)] * kinds,
        out_specs=[pl.BlockSpec(memory_space=pltpu.VMEM)] * count,
        scratch_shapes=[
            pltpu.VMEM((kinds,) + arrays[0].shape, arrays[0].dtype),
            pltpu.VMEM((kinds, head_count, shard_rows, head_size), arrays[0].dtype),
            pltpu.SemaphoreType.DMA((kinds,)),
        ],
        compiler_params=pltpu.CompilerParams(vmem_limit_bytes=40 << 20),
    )(me[None].astype(jnp.int32), *[pltpu.with_memory_space_constraint(a, pltpu.HBM) for a in arrays])


def unpack_kernel(order, copies, *refs):
    count = len(order)
    scalars = refs[0]
    ins = refs[1 : 1 + count]
    outs = refs[1 + count : 5 + count]
    heads, turned, done = refs[5 + count :]
    me = scalars[0]
    sends = []
    for t in range(4):
        for n, d in enumerate(order):
            heads[t, (me ^ d) // copies] = ins[n][t]
        turned[t] = jnp.swapaxes(heads[t], 0, 1)
        send = pltpu.make_async_copy(turned.at[t], outs[t], done.at[t])
        send.start()
        sends.append(send)
    for send in sends:
        send.wait()


def unpack(blocks, order, me, head_count):
    count = len(blocks)
    kinds, shard_rows, head_size = blocks[0].shape
    shape = (shard_rows, head_count, head_size)
    return pl.pallas_call(
        functools.partial(unpack_kernel, order, count // head_count),
        out_shape=[jax.ShapeDtypeStruct(shape, blocks[0].dtype)] * kinds,
        in_specs=[pl.BlockSpec(memory_space=pltpu.SMEM)]
        + [pl.BlockSpec(memory_space=pltpu.VMEM)] * count,
        out_specs=[pl.BlockSpec(memory_space=pltpu.HBM)] * kinds,
        scratch_shapes=[
            pltpu.VMEM((kinds, head_count, shard_rows, head_size), blocks[0].dtype),
            pltpu.VMEM((kinds,) + shape, blocks[0].dtype),
            pltpu.SemaphoreType.DMA((kinds,)),
        ],
        compiler_params=pltpu.CompilerParams(vmem_limit_bytes=40 << 20),
    )(me[None].astype(jnp.int32), *blocks)


def on_device(queries, key_vecs, value_vecs, out_grad, doc_ids):
    head_count = queries.shape[1]
    count = lax.axis_size("ctx")
    me = lax.axis_index("ctx")
    order, back = partner_orders(count)

    def exchange(blocks, order):
        got = {0: blocks[0]}
        for d in order[1:]:
            got[d] = lax.ppermute(blocks[d], "ctx", [(s, s ^ d) for s in range(count)])
        return got

    arrays = (queries, key_vecs, value_vecs, out_grad)
    mine = dict(zip(order, pack(arrays, order, me)))
    got = exchange(mine, order)
    results = attend([got[d] for d in order], order, doc_ids, me)
    returned = exchange(dict(zip(order, results)), back)
    return tuple(unpack([returned[d] for d in back], back, me, head_count))


def solution(mesh):
    spec = P(("grp", "ctx"), "head", None)
    return jax.shard_map(
        on_device,
        mesh=mesh,
        in_specs=(spec, spec, spec, spec, P("grp")),
        out_specs=(spec, spec, spec, spec),
        check_vma=False,
    )
```

```python
import functools
import math

import jax
import jax.numpy as jnp
from jax import lax
from jax.experimental import pallas as pl
from jax.experimental.pallas import tpu as pltpu
from jax.sharding import PartitionSpec as P

TILE = 256
HIDDEN = -1e30


def partner_orders(count):
    far, near = list(range(count - 1, count // 2 - 1, -1)), list(range(count // 2 - 1, 0, -1))
    first = far[count // 4 :] + far[: count // 4]
    turns = [d for pair in zip(first, near) for d in pair] + first[-1:]
    back = near + far
    return (0, *turns), (0, *back[count // 2 :], *back[: count // 2])


def nt_dot(a, b):
    return lax.dot_general(a, b, (((1,), (1,)), ((), ())), preferred_element_type=jnp.float32)


def dot(a, b):
    return jnp.dot(a, b, preferred_element_type=jnp.float32)


def attention_kernel(order, tile_most, *refs):
    count = len(order)
    scalars, start_ref = refs[0], refs[1]
    ins = refs[2 : 2 + count]
    outs = refs[2 + count : 2 + 2 * count]
    rows, key_t, value_t, scores, weights, dweights, key_sum, value_sum, result = refs[2 + 2 * count :]
    me = scalars[0]
    shard_rows = ins[0].shape[1]
    half = shard_rows // 2
    tokens = rows.shape[1]
    head_size = rows.shape[2]
    tile = TILE
    scaling = head_size ** (-0.5)
    longest = tokens * 5 // 8
    exponent = scaling * math.log2(math.e)

    for n, d in enumerate(order):
        shard = me ^ d
        low = pl.multiple_of(shard * half, half)
        high = pl.multiple_of((2 * count - 1 - shard) * half, half)
        for t in range(4):
            rows[t, pl.ds(low, half), :] = ins[n][t, :half, :]
            rows[t, pl.ds(high, half), :] = ins[n][t, half:, :]
    for b in range(tokens // tile):
        block = pl.ds(b * tile, tile)
        key_t[:, block] = rows[1, block, :].T
        value_t[:, block] = rows[2, block, :].T
    key_sum[...] = jnp.zeros_like(key_sum)
    value_sum[...] = jnp.zeros_like(value_sum)

    wide = 2 * tile

    def query_tile(size, j):
        q_at = j * wide
        k_at = q_at + wide - size * tile
        q_blk = rows[0, pl.ds(q_at, wide), :]
        start = start_ref[:, pl.ds(q_at, wide)]
        query_tb = q_blk.T

        def cols(i):
            if i == size - 1:
                return slice(tile, wide)
            gap = q_at + tile - (k_at + (i + 1) * tile - 1)
            return slice(0, tile) if gap > longest - 1 else slice(0, wide)

        def join(i, old, new, f):
            c = cols(i)
            parts = [old[:, : c.start], f(old[:, c], new), old[:, c.stop :]]
            return jnp.concatenate([p for p in parts if p.shape[1]], 1)

        best = jnp.full((1, wide), HIDDEN, jnp.float32)
        for i in range(size):
            c = cols(i)
            n = c.stop - c.start
            s = dot(rows[1, pl.ds(k_at + i * tile, tile), :], query_tb[:, c]) * exponent
            k_pos = lax.broadcasted_iota(jnp.int32, (tile, n), 0) + (k_at + i * tile)
            seen = k_pos >= start[:, c]
            if i >= size - 2:
                q_pos = lax.broadcasted_iota(jnp.int32, (tile, n), 1) + (q_at + c.start)
                seen = seen & (k_pos <= q_pos)
            s = jnp.where(seen, s, HIDDEN)
            scores[i * tile : (i + 1) * tile, c] = s
            top = jnp.max(s, axis=0, keepdims=True)
            best = join(i, best, top, jnp.maximum)
        total = jnp.zeros((1, wide), jnp.float32)
        for i in range(size):
            c = cols(i)
            e = jnp.exp2(scores[i * tile : (i + 1) * tile, c] - best[:, c])
            part = jnp.sum(e, axis=0, keepdims=True)
            total = join(i, total, part, jnp.add)
            if c.stop < wide:
                blank = jnp.zeros((tile, wide - c.stop), jnp.bfloat16)
                weights[i * tile : (i + 1) * tile, c.stop :] = blank
                dweights[i * tile : (i + 1) * tile, c.stop :] = blank
            weights[i * tile : (i + 1) * tile, c] = e.astype(jnp.bfloat16)
        inverse = 1.0 / total
        body = size - 1
        out_t = dot(value_t[:, pl.ds(k_at, body * tile)], weights[: body * tile, :])
        last = dot(value_t[:, pl.ds(k_at + body * tile, tile)], weights[body * tile : size * tile, tile:])
        out_t = jnp.concatenate([out_t[:, :tile], out_t[:, tile:] + last], 1) * inverse
        out = out_t.astype(jnp.bfloat16)
        result[0, pl.ds(q_at, wide), :] = out_t.T.astype(jnp.bfloat16)
        grad_t = rows[3, pl.ds(q_at, wide), :].astype(jnp.float32).T * inverse
        delta = jnp.sum(grad_t * out.astype(jnp.float32), axis=0, keepdims=True)
        grad_tb = grad_t.astype(jnp.bfloat16)
        for i in range(size):
            c = cols(i)
            keys = pl.ds(k_at + i * tile, tile)
            e = weights[i * tile : (i + 1) * tile, c]
            value_sum[:, keys] += nt_dot(grad_tb[:, c], e)
            dprobs = dot(rows[2, keys, :], grad_tb[:, c])
            ds = (e.astype(jnp.float32) * (dprobs - delta[:, c])).astype(jnp.bfloat16)
            dweights[i * tile : (i + 1) * tile, c] = ds
        for i in range(size):
            c = cols(i)
            keys = pl.ds(k_at + i * tile, tile)
            key_sum[:, keys] += nt_dot(query_tb[:, c], dweights[i * tile : (i + 1) * tile, c])
        query_t = dot(key_t[:, pl.ds(k_at, body * tile)], dweights[: body * tile, :])
        last = dot(key_t[:, pl.ds(k_at + body * tile, tile)], dweights[body * tile : size * tile, tile:])
        query_t = jnp.concatenate([query_t[:, :tile], query_t[:, tile:] + last], 1)
        result[1, pl.ds(q_at, wide), :] = (query_t * scaling).T.astype(jnp.bfloat16)

    for j in range(tokens // wide):
        query_tile(min(2 * j + 2, tile_most), j)

    for b in range(tokens // tile):
        block = pl.ds(b * tile, tile)
        result[2, block, :] = (key_sum[:, block] * scaling).T.astype(jnp.bfloat16)
        result[3, block, :] = value_sum[:, block].T.astype(jnp.bfloat16)
    for n, d in enumerate(order):
        shard = me ^ d
        low = pl.multiple_of(shard * half, half)
        high = pl.multiple_of((2 * count - 1 - shard) * half, half)
        for t in range(4):
            outs[n][t, :half, :] = result[t, pl.ds(low, half), :]
            outs[n][t, half:, :] = result[t, pl.ds(high, half), :]


def attend(blocks, order, doc_ids, me):
    count = len(blocks)
    tokens = doc_ids.shape[0]
    head_size = blocks[0].shape[2]
    tiles = tokens // TILE
    longest = tokens * 5 // 8
    tile_most = min(tiles, 2 + -(-(longest - 1) // TILE))
    start = jnp.sum((doc_ids[:, None] < doc_ids[None, :]).astype(jnp.int32), axis=0)
    scalars = me[None].astype(jnp.int32)
    span = tile_most * TILE
    return pl.pallas_call(
        functools.partial(attention_kernel, order, tile_most),
        out_shape=[jax.ShapeDtypeStruct(b.shape, b.dtype) for b in blocks],
        in_specs=[pl.BlockSpec(memory_space=pltpu.SMEM)]
        + [pl.BlockSpec(memory_space=pltpu.VMEM)] * (count + 1),
        out_specs=[pl.BlockSpec(memory_space=pltpu.VMEM)] * count,
        scratch_shapes=[
            pltpu.VMEM((4, tokens, head_size), jnp.bfloat16),
            pltpu.VMEM((head_size, tokens), jnp.bfloat16),
            pltpu.VMEM((head_size, tokens), jnp.bfloat16),
            pltpu.VMEM((span, 2 * TILE), jnp.float32),
            pltpu.VMEM((span, 2 * TILE), jnp.bfloat16),
            pltpu.VMEM((span, 2 * TILE), jnp.bfloat16),
            pltpu.VMEM((head_size, tokens), jnp.float32),
            pltpu.VMEM((head_size, tokens), jnp.float32),
            pltpu.VMEM((4, tokens, head_size), jnp.bfloat16),
        ],
        compiler_params=pltpu.CompilerParams(vmem_limit_bytes=40 << 20),
    )(scalars, start[None, :], *blocks)


def pack_kernel(order, copies, *refs):
    count = len(order)
    scalars = refs[0]
    ins = refs[1:5]
    outs = refs[5 : 5 + count]
    held, heads, done = refs[5 + count :]
    me = scalars[0]
    loads = [pltpu.make_async_copy(ins[t], held.at[t], done.at[t]) for t in range(4)]
    for load in loads:
        load.start()
    for t in range(4):
        loads[t].wait()
        heads[t] = jnp.swapaxes(held[t], 0, 1)
        for n, d in enumerate(order):
            outs[n][t] = heads[t, (me ^ d) // copies]


def pack(arrays, order, me):
    count = len(order)
    shard_rows, head_count, head_size = arrays[0].shape
    kinds = len(arrays)
    return pl.pallas_call(
        functools.partial(pack_kernel, order, count // head_count),
        out_shape=[jax.ShapeDtypeStruct((kinds, shard_rows, head_size), arrays[0].dtype)] * count,
        in_specs=[pl.BlockSpec(memory_space=pltpu.SMEM)]
        + [pl.BlockSpec(memory_space=pltpu.HBM)] * kinds,
        out_specs=[pl.BlockSpec(memory_space=pltpu.VMEM)] * count,
        scratch_shapes=[
            pltpu.VMEM((kinds,) + arrays[0].shape, arrays[0].dtype),
            pltpu.VMEM((kinds, head_count, shard_rows, head_size), arrays[0].dtype),
            pltpu.SemaphoreType.DMA((kinds,)),
        ],
        compiler_params=pltpu.CompilerParams(vmem_limit_bytes=40 << 20),
    )(me[None].astype(jnp.int32), *[pltpu.with_memory_space_constraint(a, pltpu.HBM) for a in arrays])


def unpack_kernel(order, copies, *refs):
    count = len(order)
    scalars = refs[0]
    ins = refs[1 : 1 + count]
    outs = refs[1 + count : 5 + count]
    heads, turned, done = refs[5 + count :]
    me = scalars[0]
    sends = []
    for t in range(4):
        for n, d in enumerate(order):
            heads[t, (me ^ d) // copies] = ins[n][t]
        turned[t] = jnp.swapaxes(heads[t], 0, 1)
        send = pltpu.make_async_copy(turned.at[t], outs[t], done.at[t])
        send.start()
        sends.append(send)
    for send in sends:
        send.wait()


def unpack(blocks, order, me, head_count):
    count = len(blocks)
    kinds, shard_rows, head_size = blocks[0].shape
    shape = (shard_rows, head_count, head_size)
    return pl.pallas_call(
        functools.partial(unpack_kernel, order, count // head_count),
        out_shape=[jax.ShapeDtypeStruct(shape, blocks[0].dtype)] * kinds,
        in_specs=[pl.BlockSpec(memory_space=pltpu.SMEM)]
        + [pl.BlockSpec(memory_space=pltpu.VMEM)] * count,
        out_specs=[pl.BlockSpec(memory_space=pltpu.HBM)] * kinds,
        scratch_shapes=[
            pltpu.VMEM((kinds, head_count, shard_rows, head_size), blocks[0].dtype),
            pltpu.VMEM((kinds,) + shape, blocks[0].dtype),
            pltpu.SemaphoreType.DMA((kinds,)),
        ],
        compiler_params=pltpu.CompilerParams(vmem_limit_bytes=40 << 20),
    )(me[None].astype(jnp.int32), *blocks)


def on_device(queries, key_vecs, value_vecs, out_grad, doc_ids):
    head_count = queries.shape[1]
    count = lax.axis_size("ctx")
    me = lax.axis_index("ctx")
    order, back = partner_orders(count)

    def exchange(blocks, order):
        got = {0: blocks[0]}
        for d in order[1:]:
            got[d] = lax.ppermute(blocks[d], "ctx", [(s, s ^ d) for s in range(count)])
        return got

    arrays = (queries, key_vecs, value_vecs, out_grad)
    mine = dict(zip(order, pack(arrays, order, me)))
    got = exchange(mine, order)
    results = attend([got[d] for d in order], order, doc_ids, me)
    returned = exchange(dict(zip(order, results)), back)
    return tuple(unpack([returned[d] for d in back], back, me, head_count))


def solution(mesh):
    spec = P(("grp", "ctx"), "head", None)
    return jax.shard_map(
        on_device,
        mesh=mesh,
        in_specs=(spec, spec, spec, spec, P("grp")),
        out_specs=(spec, spec, spec, spec),
        check_vma=False,
    )
```
